256 devices in a mesh: group: 32 (over x, z), local: 4 (over y), rep: 2 (over core).
Axes of the slice: x: 4, y: 4, z: 8, core: 2. Of those that a mesh axis runs over, the one named last changes fastest.
Arguments:
- tokens: bfloat16 [16384, 2560], P(('rep', 'group', 'local')), parts along dimension 0, may hold values from -6 to 6
- gates: bfloat16 [16384, 8], P(('rep', 'group', 'local')), parts along dimension 0, may hold values from 0.049804688 to 1
- expert_ids: int32 [16384, 8], P(('rep', 'group', 'local')), parts along dimension 0, may hold values from 0 to 127, as said below
- w_gate: bfloat16 [128, 2560, 768], P(('group', 'local')), may hold values from -0.125 to 0.125
- w_up: bfloat16 [128, 2560, 768], P(('group', 'local')), may hold values from -0.125 to 0.125
- w_down: bfloat16 [128, 768, 2560], P(('group', 'local')), may hold values from -0.21875 to 0.21875
Outputs:
- mixed: bfloat16 [16384, 2560], P(('rep', 'group', 'local')), parts along dimension 0
The draws below stay inside these ranges and needn't reach their ends.
There are 2 independent parts, one for each index of `rep`. The reference program is written for one: setup_inputs(seed, part) draws one part's arguments, and reference() takes and returns one part's arrays. A program takes and returns all parts, laid end to end along the dimension named above; an argument that names none is the same for every part. Nothing has to cross between parts.
Inputs may be any that keep to these rules, and one draw needn't show every extreme that they name: `expert_ids`: each row names 8 different experts, which lie in at most 4 groups (expert // 4).
All inputs are finite; a program needn't handle non-finite values.
Results may differ from the reference program's by a relative error of at most 0.0057.
Values may be sent and summed in bfloat16 or wider, within the bound.
A program may use at most 64 MiB of HBM per device.

```python
import math
import jax
import jax.numpy as jnp
from jax import lax

D = 2560
FF = 768
TOP = 8
GROUPS_TOK = 4
TOK_DEV = 64
GROUPS = 32
EXP_GROUP = 4
EXPERTS = 128
TOKENS = 8192
PAIR_CAP = 8


def draw_expert_ids(key, part):
    key_hot, key_group, key_ehot, key_expert = jax.random.split(key, 4)
    group_hot = jax.random.randint(key_hot, (GROUPS,), 0, 3000)
    group_affinity = jax.random.randint(key_group, (TOKENS, GROUPS), 0, 4000) + group_hot
    group_affinity = group_affinity * 128 + jnp.arange(GROUPS, dtype=jnp.int32)
    _, picked_groups = lax.top_k(group_affinity, GROUPS_TOK)
    candidate_experts = (picked_groups[:, :, None] * EXP_GROUP + jnp.arange(EXP_GROUP, dtype=jnp.int32)).reshape(TOKENS, GROUPS_TOK * EXP_GROUP)
    expert_hot = jax.random.randint(key_ehot, (EXPERTS,), 0, 3000)
    expert_affinity = jax.random.randint(key_expert, (TOKENS, GROUPS_TOK * EXP_GROUP), 0, 4000) + expert_hot[candidate_experts]
    expert_affinity = expert_affinity * 256 + jnp.arange(GROUPS_TOK * EXP_GROUP, dtype=jnp.int32)
    _, picks = lax.top_k(expert_affinity, TOP)
    return jnp.take_along_axis(candidate_experts, picks, axis=1).astype(jnp.int32)


def level_of(key, dims, pieces, low, largest):
    def one(axis_at, parts):
        steps = jax.random.uniform(jax.random.fold_in(jax.random.fold_in(key, 6), axis_at), (parts,), jnp.float32, low / len(pieces), largest / len(pieces))
        return jnp.repeat(jnp.exp(steps), dims[axis_at] // parts).reshape((-1,) + (1,) * (len(dims) - axis_at - 1))

    gain = one(*pieces[0])
    for cut in pieces[1:]:
        gain = gain * one(*cut)
    return gain


def scatter_about(stream_key, shape, deviation, reach, cuts=(), kind=jnp.bfloat16):
    factor_of = level_of(stream_key, shape, cuts, -0.22, 0.18) if cuts else 1.0
    drawn = jax.random.normal(stream_key, shape, jnp.float32) * deviation * factor_of
    return jnp.minimum(jnp.maximum(drawn, -reach), reach).astype(kind)


def setup_inputs(seed: int = 0, part: int = 0) -> dict:
    arg_keys = jax.random.split(jax.random.key(seed), 7)
    part_splits = jax.random.split(jax.random.fold_in(arg_keys[6], part), 7)
    tokens = scatter_about(part_splits[0], (TOKENS, D), 1.0, 6.0, ((0, 128),))
    gates = jnp.clip(jnp.exp(math.log(1.0) - 2.9996462 * jax.random.uniform(part_splits[1], (TOKENS, TOP), jnp.float32) ** level_of(part_splits[1], (TOKENS, TOP), ((0, 128),), -0.2, 0.2)), 0.049804688, 1.0).astype(jnp.bfloat16)
    expert_ids = draw_expert_ids(jax.random.fold_in(jax.random.fold_in(arg_keys[6], part), 71), part)
    w_gate = scatter_about(arg_keys[3], (EXPERTS, D, FF), D ** -0.5, 0.125, ((0, 128),))
    w_up = scatter_about(arg_keys[4], (EXPERTS, D, FF), D ** -0.5, 0.125, ((0, 128),))
    w_down = scatter_about(arg_keys[5], (EXPERTS, FF, D), FF ** -0.5, 0.21875, ((0, 128),))
    return dict(tokens=tokens, gates=gates, expert_ids=expert_ids, w_gate=w_gate, w_up=w_up, w_down=w_down)


def expert_rows(rows, gate_mat, up_mat, down_mat):
    gate = jnp.dot(rows, gate_mat, preferred_element_type=jnp.float32)
    up = jnp.dot(rows, up_mat, preferred_element_type=jnp.float32)
    hidden = (jax.nn.silu(gate) * up).astype(jnp.bfloat16)
    return jnp.dot(hidden, down_mat, preferred_element_type=jnp.float32).astype(jnp.bfloat16)


def reference(tokens, gates, expert_ids, w_gate, w_up, w_down):
    blocks = GROUPS * EXP_GROUP
    input_rows = tokens.reshape(blocks, TOK_DEV, D)
    chosen = expert_ids.reshape(blocks, TOK_DEV, TOP)
    gate_vals = gates.reshape(blocks, TOK_DEV, TOP).astype(jnp.float32)
    expert_iota = jnp.arange(EXPERTS, dtype=jnp.int32)
    hits = chosen[..., None] == expert_iota
    weights = jnp.sum(jnp.where(hits, gate_vals[..., None], jnp.float32(0.0)), axis=2)
    member = jnp.any(jnp.any(hits, axis=2).reshape(blocks, TOK_DEV, GROUPS, EXP_GROUP), axis=3).astype(jnp.int32)
    rank = jnp.cumsum(member, axis=1) - member
    slot_iota = jnp.arange(PAIR_CAP, dtype=jnp.int32)
    place = ((member[..., None] == 1) & (rank[..., None] == slot_iota)).astype(jnp.float32)
    dispatched = jnp.einsum("stgc,std->sgcd", place, input_rows.astype(jnp.float32)).astype(jnp.bfloat16)
    slot_weights = jnp.einsum("stgc,stgl->sgcl", place, weights.reshape(blocks, TOK_DEV, GROUPS, EXP_GROUP), precision=lax.Precision.HIGHEST)

    def step(total, expert):
        group_idx = (expert // EXP_GROUP).astype(jnp.int32)
        local_idx = (expert % EXP_GROUP).astype(jnp.int32)
        rows = lax.dynamic_index_in_dim(dispatched, group_idx, 1, keepdims=False).reshape(blocks * PAIR_CAP, D)
        outputs = expert_rows(rows, lax.dynamic_index_in_dim(w_gate, expert, 0, keepdims=False), lax.dynamic_index_in_dim(w_up, expert, 0, keepdims=False), lax.dynamic_index_in_dim(w_down, expert, 0, keepdims=False))
        group_w = lax.dynamic_index_in_dim(slot_weights, group_idx, 1, keepdims=False)
        expert_w = lax.dynamic_index_in_dim(group_w, local_idx, 2, keepdims=False)
        terms = expert_w[..., None] * outputs.reshape(blocks, PAIR_CAP, D).astype(jnp.float32)
        group_place = lax.dynamic_index_in_dim(place, group_idx, 2, keepdims=False)
        total = total + jnp.einsum("stc,scd->std", group_place, terms, precision=lax.Precision.HIGHEST)
        return total, None

    start = jnp.zeros((blocks, TOK_DEV, D), jnp.float32)
    total, _ = lax.scan(step, start, jnp.arange(EXPERTS, dtype=jnp.int32))
    return total.reshape(TOKENS, D).astype(jnp.bfloat16)
```

```python
import functools

import jax
import jax.numpy as jnp
from jax import lax
from jax.experimental import pallas as pl
from jax.experimental.pallas import tpu as pltpu
from jax.sharding import PartitionSpec as P

MESH = pl.DeviceIdType.MESH
GROUPS_TOK = 4
RING_Z = 8
LANES = 128
BLOCKS_CHUNK = 8


def tile_of(size, most):
    tile = min(size, most)
    while size % tile:
        tile -= LANES
    return tile


def layer_kernel(
    cfg,
    tok_ref, ids_ref, gates_ref, wg_hbm, wu_hbm, wd_hbm,
    out_ref,
    wg, wu, wd, sent, place_ref, rows, wcol, hidden, part, half_in, full_in, back, returned,
    w_sem, a_send, a_recv, d_send, d_recv, f_send, f_recv, p_send, p_recv, q_send, q_recv, b_send, b_recv,
):
    n_group, cap, nz, nb, chunks, width, ff = cfg
    nx = n_group // nz
    n_tok = tok_ref.shape[0]
    part_rows = nb * cap
    half = part_rows // 2
    slots = n_group * cap
    f32, bf16 = jnp.float32, jnp.bfloat16

    me = lax.axis_index("group")
    mx, mz = me // nz, lax.rem(me, nz)
    my = lax.axis_index("local")
    right, left = lax.rem(my + 1, 4), lax.rem(my + 3, 4)

    def forth(j):
        return lax.rem(mx + j // nz, nx) * nz + lax.rem(mz + lax.rem(j, nz), nz)

    def origin(j):
        return lax.rem(mx + nx - j // nz, nx) * nz + lax.rem(mz + nz - lax.rem(j, nz), nz)

    barrier = pltpu.get_barrier_semaphore()

    def greet(j, carry):
        pl.semaphore_signal(barrier, inc=1, device_id={"group": forth(j)}, device_id_type=MESH)
        return carry

    lax.fori_loop(1, n_group, greet, 0)
    pl.semaphore_signal(barrier, inc=1, device_id={"local": right}, device_id_type=MESH)
    pl.semaphore_signal(barrier, inc=1, device_id={"local": left}, device_id_type=MESH)

    loads = [
        pltpu.make_async_copy(hbm.at[0], vmem, w_sem.at[i])
        for i, (hbm, vmem) in enumerate(((wg_hbm, wg), (wu_hbm, wu), (wd_hbm, wd)))
    ]
    for load in loads:
        load.start()

    expert_at = lax.broadcasted_iota(jnp.int32, (LANES, n_tok), 0)
    hit = jnp.zeros((LANES, n_tok), f32)
    weight = jnp.zeros((LANES, n_tok), f32)
    for k in range(ids_ref.shape[0]):
        same = ids_ref[k : k + 1, :] == expert_at
        hit = jnp.where(same, 1.0, hit)
        weight = jnp.where(same, gates_ref[k : k + 1, :].astype(f32), weight)
    slot_at = lax.broadcasted_iota(jnp.int32, (slots, LANES), 0)
    of_expert = lax.broadcasted_iota(jnp.int32, (slots, LANES), 1)
    in_group = jnp.where(slot_at // cap == of_expert // 4, 1.0, 0.0).astype(bf16)
    count = jnp.dot(in_group, hit.astype(bf16), preferred_element_type=f32)
    member = jnp.where(count > 0.5, 1.0, 0.0)
    t_row = lax.broadcasted_iota(jnp.int32, (n_tok, n_tok), 0)
    t_col = lax.broadcasted_iota(jnp.int32, (n_tok, n_tok), 1)
    before = jnp.where(t_row < t_col, 1.0, 0.0).astype(bf16)
    rank = jnp.dot(member.astype(bf16), before, preferred_element_type=f32)
    slot_rank = lax.rem(lax.broadcasted_iota(jnp.int32, (slots, n_tok), 0), cap).astype(f32)
    place = jnp.where((count > 0.5) & (rank == slot_rank), 1.0, 0.0).astype(bf16)
    across = (((1,), (1,)), ((), ()))
    same_tok = jnp.where(t_row == t_col, 1.0, 0.0).astype(bf16)
    place_ref[...] = lax.dot_general(same_tok, place, across, preferred_element_type=f32).astype(bf16)
    sent[:, width:] = lax.dot_general(
        place, weight.astype(bf16), across, preferred_element_type=f32
    ).astype(bf16)
    cols = tile_of(width, 512)

    def gather_cols(n, carry):
        at = pl.ds(pl.multiple_of(n * cols, cols), cols)
        sent[:, at] = jnp.dot(place, tok_ref[:, at], preferred_element_type=f32).astype(bf16)
        return carry

    lax.fori_loop(0, width // cols, gather_cols, 0)
    pl.semaphore_wait(barrier, n_group + 1)

    def block(ref, index):
        return ref.at[pl.ds(pl.multiple_of(index * cap, cap), cap), :]

    def dispatch(j):
        target = forth(j)
        return pltpu.make_async_remote_copy(
            src_ref=block(sent, target),
            dst_ref=block(rows.at[j // nb], lax.rem(j, nb)),
            send_sem=a_send.at[j],
            recv_sem=a_recv.at[j],
            device_id={"group": target},
            device_id_type=MESH,
        )

    def give_back(j):
        return pltpu.make_async_remote_copy(
            src_ref=block(back.at[j // nb], lax.rem(j, nb)),
            dst_ref=block(returned, me),
            send_sem=b_send.at[j],
            recv_sem=b_recv.at[j],
            device_id={"group": origin(j)},
            device_id_type=MESH,
        )

    own_in = pltpu.make_async_copy(block(sent, me), rows.at[0, pl.ds(0, cap), :], a_recv.at[0])
    own_in.start()

    def start_dispatch(j, carry):
        dispatch(j).start()
        return carry

    lax.fori_loop(1, n_group, start_dispatch, 0)

    def copy_y(src, dst, send, recv, side):
        return pltpu.make_async_remote_copy(
            src_ref=src, dst_ref=dst, send_sem=send, recv_sem=recv,
            device_id={"local": right if side == 0 else left}, device_id_type=MESH,
        )

    def piece(ref, c, begin, size):
        return ref.at[c, pl.ds(begin, size), :]

    n1, n2, n3 = part_rows, 2 * part_rows, 3 * part_rows

    def direct(c, side):
        return copy_y(piece(rows, c, 0, n1), piece(rows, c, (n3, n1)[side], n1),
                      d_send.at[c, side], d_recv.at[c, side], side)

    def onward(c, side):
        return copy_y(piece(rows, c, (n3, n1 + half)[side], half), piece(rows, c, (n2, n2 + half)[side], half),
                      f_send.at[c, side], f_recv.at[c, side], side)

    def far(c, side):
        return copy_y(piece(part, c, (n2, n2 + half)[side], half), half_in.at[c, side],
                      p_send.at[c, side], p_recv.at[c, side], side)

    def near(c, side, which):
        begin = (half if which == 0 else 0) if side == 0 else (0 if which == 0 else half)
        return copy_y(piece(part, c, (n1, n3)[side] + begin, half), full_in.at[c, side, pl.ds(begin, half), :],
                      q_send.at[c, 2 * which + side], q_recv.at[c, 2 * which + side], side)

    fcols = tile_of(ff, 256)
    dcols = tile_of(width, 512)

    def compute(c):
        lane = lax.broadcasted_iota(jnp.int32, (4 * part_rows, LANES), 1)
        gate_of = rows[c, :, width:].astype(f32)
        mine = jnp.sum(jnp.where(lane == me * 4 + my, gate_of, 0.0), axis=1, keepdims=True)
        wcol[...] = jnp.broadcast_to(mine, (4 * part_rows, LANES))

        def up_cols(n, carry):
            at = pl.ds(pl.multiple_of(n * fcols, fcols), fcols)
            x = rows[c, :, :width]
            gate = jnp.dot(x, wg[:, at], preferred_element_type=f32)
            up = jnp.dot(x, wu[:, at], preferred_element_type=f32)
            hidden[:, at] = (gate / (1.0 + jnp.exp(-gate)) * up).astype(bf16)
            return carry

        lax.fori_loop(0, ff // fcols, up_cols, 0)

        def down_cols(n, carry):
            at = pl.ds(pl.multiple_of(n * dcols, dcols), dcols)
            value = jnp.dot(hidden[...], wd[:, at], preferred_element_type=f32)
            part[c, :, at] = (value * wcol[:, 0:1]).astype(bf16)
            return carry

        lax.fori_loop(0, width // dcols, down_cols, 0)

    def step(s, carry):
        @pl.when(s < chunks)
        def _():
            c = s

            def arrived(b, inner):
                j = c * nb + b
                pltpu.make_async_copy(block(sent, 0), block(rows.at[c], b), a_recv.at[j]).wait()
                return inner

            lax.fori_loop(0, nb, arrived, 0)
            direct(c, 0).start()
            direct(c, 1).start()

        @pl.when((s >= 1) & (s <= chunks))
        def _():
            c = s - 1
            for side in (0, 1):
                direct(c, side).wait_recv()
                onward(c, side).start()

        @pl.when((s >= 2) & (s <= chunks + 1))
        def _():
            c = s - 2

            @pl.when(c == 0)
            def _():
                for load in loads:
                    load.wait()

            for side in (0, 1):
                onward(c, side).wait_recv()
            compute(c)
            for side in (0, 1):
                far(c, side).start()
            for side in (0, 1):
                near(c, side, 0).start()

        @pl.when((s >= 3) & (s <= chunks + 2))
        def _():
            c = s - 3
            for side in (0, 1):
                far(c, side).wait_recv()
                at = pl.ds((n1, n3 + half)[side], half)
                part[c, at, :] = (part[c, at, :].astype(f32) + half_in[c, side].astype(f32)).astype(bf16)
                near(c, side, 1).start()

        @pl.when(s >= 4)
        def _():
            c = s - 4
            for which in (0, 1):
                for side in (0, 1):
                    near(c, side, which).wait_recv()
            back[c] = (
                part[c, pl.ds(0, n1), :].astype(f32)
                + full_in[c, 0].astype(f32)
                + full_in[c, 1].astype(f32)
            ).astype(bf16)

            def send_back(b, inner):
                j = c * nb + b

                @pl.when(j == 0)
                def _():
                    pltpu.make_async_copy(block(back.at[0], 0), block(returned, me), b_recv.at[0]).start()

                @pl.when(j != 0)
                def _():
                    give_back(j).start()

                return inner

            lax.fori_loop(0, nb, send_back, 0)

        return carry

    lax.fori_loop(0, chunks + 4, step, 0)

    def sends_done(c, carry):
        for side in (0, 1):
            direct(c, side).wait_send()
            onward(c, side).wait_send()
            far(c, side).wait_send()
            near(c, side, 0).wait_send()
            near(c, side, 1).wait_send()
        return carry

    lax.fori_loop(0, chunks, sends_done, 0)

    def blocks_done(j, carry):
        dispatch(j).wait_send()
        give_back(j).wait_send()
        return carry

    lax.fori_loop(1, n_group, blocks_done, 0)

    def came_back(j, carry):
        pltpu.make_async_copy(block(back.at[0], 0), block(returned, forth(j)), b_recv.at[j]).wait()
        return carry

    lax.fori_loop(0, n_group, came_back, 0)

    def mix_cols(n, carry):
        at = pl.ds(pl.multiple_of(n * cols, cols), cols)
        out_ref[:, at] = jnp.dot(place_ref[...], returned[:, at], preferred_element_type=f32).astype(bf16)
        return carry

    lax.fori_loop(0, width // cols, mix_cols, 0)


def shards(ring_z, blocks_chunk, tokens, gates, expert_ids, w_gate, w_up, w_down):
    n_tok, width = tokens.shape
    n_group = lax.axis_size("group")
    ff = w_gate.shape[2]
    cap = min(n_tok, n_tok * GROUPS_TOK // n_group)
    nb = blocks_chunk
    chunks = n_group // nb
    n1 = nb * cap
    bf16 = jnp.bfloat16
    vmem = pl.BlockSpec(memory_space=pltpu.VMEM)
    hbm = pl.BlockSpec(memory_space=pl.ANY)
    dma = pltpu.SemaphoreType.DMA
    cfg = (n_group, cap, ring_z, nb, chunks, width, ff)
    return pl.pallas_call(
        functools.partial(layer_kernel, cfg),
        out_shape=jax.ShapeDtypeStruct((n_tok, width), bf16),
        in_specs=[vmem, vmem, vmem, hbm, hbm, hbm],
        out_specs=vmem,
        scratch_shapes=[
            pltpu.VMEM((width, ff), bf16),
            pltpu.VMEM((width, ff), bf16),
            pltpu.VMEM((ff, width), bf16),
            pltpu.VMEM((n_group * cap, width + LANES), bf16),
            pltpu.VMEM((n_tok, n_group * cap), bf16),
            pltpu.VMEM((chunks, 4 * n1, width + LANES), bf16),
            pltpu.VMEM((4 * n1, LANES), jnp.float32),
            pltpu.VMEM((4 * n1, ff), bf16),
            pltpu.VMEM((chunks, 4 * n1, width), bf16),
            pltpu.VMEM((chunks, 2, n1 // 2, width), bf16),
            pltpu.VMEM((chunks, 2, n1, width), bf16),
            pltpu.VMEM((chunks, n1, width), bf16),
            pltpu.VMEM((n_group * cap, width), bf16),
            dma((3,)),
            dma((n_group,)), dma((n_group,)),
            dma((chunks, 2)), dma((chunks, 2)),
            dma((chunks, 2)), dma((chunks, 2)),
            dma((chunks, 2)), dma((chunks, 2)),
            dma((chunks, 4)), dma((chunks, 4)),
            dma((n_group,)), dma((n_group,)),
        ],
        compiler_params=pltpu.CompilerParams(
            collective_id=0, has_side_effects=True, vmem_limit_bytes=60 * 1024 * 1024
        ),
        name="moe_layer",
    )(tokens, expert_ids.T, gates.T, w_gate, w_up, w_down)


def solution(mesh):
    in_specs = (
        P(("rep", "group", "local"), None),
        P(("rep", "group", "local"), None),
        P(("rep", "group", "local"), None),
        P(("group", "local"), None, None),
        P(("group", "local"), None, None),
        P(("group", "local"), None, None),
    )
    out_specs = P(("rep", "group", "local"), None)
    return jax.shard_map(
        functools.partial(shards, RING_Z, BLOCKS_CHUNK),
        mesh=mesh, in_specs=in_specs, out_specs=out_specs, check_vma=False,
    )
```

```python
import functools

import jax
import jax.numpy as jnp
from jax import lax
from jax.experimental import pallas as pl
from jax.experimental.pallas import tpu as pltpu
from jax.sharding import PartitionSpec as P

MESH = pl.DeviceIdType.MESH
GROUPS_TOK = 4
RING_Z = 8
LANES = 128
LAGS = (1, 2, 3, 4)
BLOCKS_CHUNK = 4


def tile_of(size, most):
    tile = min(size, most)
    while size % tile:
        tile -= LANES
    return tile


def layer_kernel(
    cfg,
    tok_ref, ids_ref, gates_ref, wg_hbm, wu_hbm, wd_hbm,
    out_ref,
    wg, wu, wd, sent, sent_gates, place_ref, rows, gates_in, packed, wcol, hidden, part, half_in, full_in, back, returned,
    wide_sem, w_sem, a_send, a_recv, h_send, h_recv, d_send, d_recv, f_send, f_recv, g_send, g_recv, p_send, p_recv, q_send, q_recv, b_send, b_recv,
):
    n_group, cap, nz, nb, chunks, width, ff = cfg
    nx = n_group // nz
    n_tok = tok_ref.shape[0]
    part_rows = nb * cap
    half = part_rows // 2
    slots = n_group * cap
    f32, bf16 = jnp.float32, jnp.bfloat16

    me = lax.axis_index("group")
    mx, mz = me // nz, lax.rem(me, nz)
    my = lax.axis_index("local")
    right, left = lax.rem(my + 1, 4), lax.rem(my + 3, 4)

    def lane_block(group):
        dx, dz = lax.rem(group // nz + nx - mx, nx), lax.rem(lax.rem(group, nz) + nz - mz, nz)
        if (nx, nz) != (4, 8):
            return lax.rem(dx * nz + dz, nb)
        split = jnp.minimum(lax.rem(dz, 4), 1)
        b = (1 - split) * dx + split * (2 * lax.rem(dx, 2) + dz // 4)
        return b

    def offset(j):
        if (nx, nz) != (4, 8):
            return j // nz, lax.rem(j, nz)
        c, b = j // 4, lax.rem(j, 4)
        both = (lax.rem(c, 4) + 3) // 4
        dx = (1 - both) * b + both * (b // 2 + 2 * (c // 4))
        return dx, (4 - jnp.abs(c - 4)) * (1 - 2 * lax.rem(b, 2))

    def forth(j):
        dx, dz = offset(j)
        return lax.rem(mx + dx, nx) * nz + lax.rem(mz + dz + nz, nz)

    def origin(j):
        dx, dz = offset(j)
        return lax.rem(mx - dx + nx, nx) * nz + lax.rem(mz - dz + nz, nz)

    barrier = pltpu.get_barrier_semaphore()

    def at_group(dx, dz):
        return {"group": lax.rem(mx + dx, nx) * nz + lax.rem(mz + dz, nz)}

    ring = sorted({1, nz - 1})
    near_by = [at_group(dx, 0) for dx in range(1, nx)] + [at_group(0, dz) for dz in ring]
    near_by += [{"local": right}, {"local": left}]
    for device in near_by:
        pl.semaphore_signal(barrier, inc=1, device_id=device, device_id_type=MESH)

    def widen(k):
        for dz in ring:
            pl.semaphore_signal(wide_sem.at[k], inc=1, device_id=at_group(0, dz), device_id_type=MESH)
        pl.semaphore_wait(wide_sem.at[k], len(ring))

    loads = [
        pltpu.make_async_copy(hbm.at[0], vmem, w_sem.at[i])
        for i, (hbm, vmem) in enumerate(((wg_hbm, wg), (wu_hbm, wu), (wd_hbm, wd)))
    ]
    for load in loads:
        load.start()

    expert_at = lax.broadcasted_iota(jnp.int32, (LANES, n_tok), 0)
    hit = jnp.zeros((LANES, n_tok), f32)
    weight = jnp.zeros((LANES, n_tok), f32)
    for k in range(ids_ref.shape[0]):
        same = ids_ref[k : k + 1, :] == expert_at
        hit = jnp.where(same, 1.0, hit)
        weight = jnp.where(same, gates_ref[k : k + 1, :].astype(f32), weight)
    slot_at = lax.broadcasted_iota(jnp.int32, (slots, LANES), 0)
    of_expert = lax.broadcasted_iota(jnp.int32, (slots, LANES), 1)
    in_group = jnp.where(slot_at // cap == of_expert // 4, 1.0, 0.0).astype(bf16)
    count = jnp.dot(in_group, hit.astype(bf16), preferred_element_type=f32)
    member = jnp.where(count > 0.5, 1.0, 0.0)
    t_row = lax.broadcasted_iota(jnp.int32, (n_tok, n_tok), 0)
    t_col = lax.broadcasted_iota(jnp.int32, (n_tok, n_tok), 1)
    before = jnp.where(t_row < t_col, 1.0, 0.0).astype(bf16)
    rank = jnp.dot(member.astype(bf16), before, preferred_element_type=f32)
    slot_rank = lax.rem(lax.broadcasted_iota(jnp.int32, (slots, n_tok), 0), cap).astype(f32)
    place = jnp.where((count > 0.5) & (rank == slot_rank), 1.0, 0.0).astype(bf16)
    across = (((1,), (1,)), ((), ()))
    same_tok = jnp.where(t_row == t_col, 1.0, 0.0).astype(bf16)
    place_ref[...] = lax.dot_general(same_tok, place, across, preferred_element_type=f32).astype(bf16)
    of_slot = lax.dot_general(place, weight.astype(bf16), across, preferred_element_type=f32).astype(bf16)
    e_row = lax.broadcasted_iota(jnp.int32, (LANES, LANES), 0)
    e_lane = lax.broadcasted_iota(jnp.int32, (LANES, LANES), 1)
    to_lane = jnp.where(e_lane == lane_block(e_row // 4) * 4 + lax.rem(e_row, 4), 1.0, 0.0).astype(bf16)
    sent_gates[...] = jnp.dot(of_slot * in_group, to_lane, preferred_element_type=f32).astype(bf16)
    cols = tile_of(width, 512)

    def gather_cols(n, carry):
        at = pl.ds(pl.multiple_of(n * cols, cols), cols)
        sent[:, at] = jnp.dot(place, tok_ref[:, at], preferred_element_type=f32).astype(bf16)
        return carry

    lax.fori_loop(0, width // cols, gather_cols, 0)
    pl.semaphore_wait(barrier, len(near_by))

    def block(ref, index):
        return ref.at[pl.ds(pl.multiple_of(index * cap, cap), cap), :]

    def dispatch(j):
        target = forth(j)
        return pltpu.make_async_remote_copy(
            src_ref=block(sent, target),
            dst_ref=block(rows.at[j // nb], lax.rem(j, nb)),
            send_sem=a_send.at[j],
            recv_sem=a_recv.at[j],
            device_id={"group": target},
            device_id_type=MESH,
        )

    def dispatch_gates(j):
        target = forth(j)
        return pltpu.make_async_remote_copy(
            src_ref=block(sent_gates, target),
            dst_ref=gates_in.at[j // nb, lax.rem(j, nb)],
            send_sem=h_send.at[j],
            recv_sem=h_recv.at[j],
            device_id={"group": target},
            device_id_type=MESH,
        )

    def give_back(j):
        return pltpu.make_async_remote_copy(
            src_ref=block(back.at[j // nb], lax.rem(j, nb)),
            dst_ref=block(returned, me),
            send_sem=b_send.at[j],
            recv_sem=b_recv.at[j],
            device_id={"group": origin(j)},
            device_id_type=MESH,
        )

    own_in = pltpu.make_async_copy(block(sent, me), rows.at[0, pl.ds(0, cap), :], a_recv.at[0])
    own_in.start()
    own_gates = pltpu.make_async_copy(block(sent_gates, me), gates_in.at[0, 0], h_recv.at[0])
    own_gates.start()

    def start_dispatch(j, carry):
        dispatch(j).start()
        dispatch_gates(j).start()
        return carry

    for k in range(nz // 2 + 1):
        if k:
            widen(k - 1)
        first, last = (max(1, nx * k), nx * (k + 1)) if (nx, nz) == (4, 8) else (1, n_group if k else 1)
        last = n_group if k == nz // 2 else last
        lax.fori_loop(first, last, start_dispatch, 0)

    def copy_y(src, dst, send, recv, side):
        return pltpu.make_async_remote_copy(
            src_ref=src, dst_ref=dst, send_sem=send, recv_sem=recv,
            device_id={"local": right if side == 0 else left}, device_id_type=MESH,
        )

    def piece(ref, c, begin, size):
        return ref.at[c, pl.ds(begin, size), :]

    n1, n2, n3 = part_rows, 2 * part_rows, 3 * part_rows

    def direct(c, side):
        return copy_y(piece(rows, c, 0, n1), piece(rows, c, (n3, n1)[side], n1),
                      d_send.at[c, side], d_recv.at[c, side], side)

    def onward(c, side):
        return copy_y(piece(rows, c, (n3, n1 + half)[side], half), piece(rows, c, (n2, n2 + half)[side], half),
                      f_send.at[c, side], f_recv.at[c, side], side)

    def direct_weights(c, side):
        return copy_y(packed.at[c, 0], packed.at[c, (3, 1)[side]], g_send.at[c, side], g_recv.at[c, side], side)

    def onward_weights(c):
        return copy_y(packed.at[c, 3], packed.at[c, 2], g_send.at[c, 2], g_recv.at[c, 2], 0)

    def far(c, side):
        return copy_y(piece(part, c, (n2, n2 + half)[side], half), half_in.at[c, side],
                      p_send.at[c, side], p_recv.at[c, side], side)

    def near(c, side, which):
        begin = (half if which == 0 else 0) if side == 0 else (0 if which == 0 else half)
        return copy_y(piece(part, c, (n1, n3)[side] + begin, half), full_in.at[c, side, pl.ds(begin, half), :],
                      q_send.at[c, 2 * which + side], q_recv.at[c, 2 * which + side], side)

    fcols = tile_of(ff, 256)
    dcols = tile_of(width, 512)

    def compute(c):
        lane = lax.broadcasted_iota(jnp.int32, (cap, LANES), 1)
        for r in range(4):
            gate_of = packed[c, r].astype(f32)
            for b in range(nb):
                mine = jnp.sum(jnp.where(lane == b * 4 + my, gate_of, 0.0), axis=1, keepdims=True)
                wcol[pl.ds(r * part_rows + b * cap, cap), :] = jnp.broadcast_to(mine, (cap, LANES))

        def up_cols(n, carry):
            at = pl.ds(pl.multiple_of(n * fcols, fcols), fcols)
            x = rows[c]
            gate = jnp.dot(x, wg[:, at], preferred_element_type=f32)
            up = jnp.dot(x, wu[:, at], preferred_element_type=f32)
            hidden[:, at] = (gate / (1.0 + jnp.exp(-gate)) * up).astype(bf16)
            return carry

        lax.fori_loop(0, ff // fcols, up_cols, 0)

        def down_cols(n, carry):
            at = pl.ds(pl.multiple_of(n * dcols, dcols), dcols)
            value = jnp.dot(hidden[...], wd[:, at], preferred_element_type=f32)
            part[c, :, at] = (value * wcol[:, 0:1]).astype(bf16)
            return carry

        lax.fori_loop(0, width // dcols, down_cols, 0)

    def step(s, carry):
        @pl.when(s < chunks)
        def _():
            c = s

            def arrived(b, inner):
                j = c * nb + b
                pltpu.make_async_copy(block(sent, 0), block(rows.at[c], b), a_recv.at[j]).wait()
                return inner

            lax.fori_loop(0, nb, arrived, 0)

            def gates_arrived(b, inner):
                j = c * nb + b
                pltpu.make_async_copy(block(sent_gates, 0), gates_in.at[c, b], h_recv.at[j]).wait()
                return inner

            lax.fori_loop(0, nb, gates_arrived, 0)
            packed[c, 0] = jnp.sum(gates_in[c].astype(f32), axis=0).astype(bf16)
            for side in (0, 1):
                direct(c, side).start()
            for side in (0, 1):
                direct_weights(c, side).start()

        @pl.when((s >= LAGS[0]) & (s < chunks + LAGS[0]))
        def _():
            c = s - LAGS[0]
            for side in (0, 1):
                direct(c, side).wait_recv()
                onward(c, side).start()
            for side in (0, 1):
                direct_weights(c, side).wait_recv()
            onward_weights(c).start()

        @pl.when((s >= LAGS[1]) & (s < chunks + LAGS[1]))
        def _():
            c = s - LAGS[1]

            @pl.when(c == 0)
            def _():
                for load in loads:
                    load.wait()

            for side in (0, 1):
                onward(c, side).wait_recv()
            onward_weights(c).wait_recv()
            compute(c)
            for side in (0, 1):
                far(c, side).start()
            for side in (0, 1):
                near(c, side, 0).start()

        @pl.when((s >= LAGS[2]) & (s < chunks + LAGS[2]))
        def _():
            c = s - LAGS[2]
            for side in (0, 1):
                far(c, side).wait_recv()
                at = pl.ds((n1, n3 + half)[side], half)
                part[c, at, :] = (part[c, at, :].astype(f32) + half_in[c, side].astype(f32)).astype(bf16)
                near(c, side, 1).start()

        @pl.when(s >= LAGS[3])
        def _():
            c = s - LAGS[3]
            for which in (0, 1):
                for side in (0, 1):
                    near(c, side, which).wait_recv()
            back[c] = (
                part[c, pl.ds(0, n1), :].astype(f32)
                + full_in[c, 0].astype(f32)
                + full_in[c, 1].astype(f32)
            ).astype(bf16)

            def send_back(b, inner):
                j = c * nb + b

                @pl.when(j == 0)
                def _():
                    pltpu.make_async_copy(block(back.at[0], 0), block(returned, me), b_recv.at[0]).start()

                @pl.when(j != 0)
                def _():
                    give_back(j).start()

                return inner

            lax.fori_loop(0, nb, send_back, 0)

        return carry

    lax.fori_loop(0, chunks + LAGS[3], step, 0)

    def sends_done(c, carry):
        for side in (0, 1):
            direct(c, side).wait_send()
            direct_weights(c, side).wait_send()
            onward(c, side).wait_send()
            far(c, side).wait_send()
            near(c, side, 0).wait_send()
            near(c, side, 1).wait_send()
        onward_weights(c).wait_send()
        return carry

    lax.fori_loop(0, chunks, sends_done, 0)

    def blocks_done(j, carry):
        dispatch(j).wait_send()
        dispatch_gates(j).wait_send()
        give_back(j).wait_send()
        return carry

    lax.fori_loop(1, n_group, blocks_done, 0)

    def came_back(j, carry):
        pltpu.make_async_copy(block(back.at[0], 0), block(returned, forth(j)), b_recv.at[j]).wait()
        return carry

    lax.fori_loop(0, n_group, came_back, 0)

    def mix_cols(n, carry):
        at = pl.ds(pl.multiple_of(n * cols, cols), cols)
        out_ref[:, at] = jnp.dot(place_ref[...], returned[:, at], preferred_element_type=f32).astype(bf16)
        return carry

    lax.fori_loop(0, width // cols, mix_cols, 0)


def shards(ring_z, blocks_chunk, tokens, gates, expert_ids, w_gate, w_up, w_down):
    n_tok, width = tokens.shape
    n_group = lax.axis_size("group")
    ff = w_gate.shape[2]
    cap = min(n_tok, n_tok * GROUPS_TOK // n_group)
    nb = blocks_chunk
    chunks = n_group // nb
    n1 = nb * cap
    bf16 = jnp.bfloat16
    vmem = pl.BlockSpec(memory_space=pltpu.VMEM)
    hbm = pl.BlockSpec(memory_space=pl.ANY)
    dma = pltpu.SemaphoreType.DMA
    cfg = (n_group, cap, ring_z, nb, chunks, width, ff)
    return pl.pallas_call(
        functools.partial(layer_kernel, cfg),
        out_shape=jax.ShapeDtypeStruct((n_tok, width), bf16),
        in_specs=[vmem, vmem, vmem, hbm, hbm, hbm],
        out_specs=vmem,
        scratch_shapes=[
            pltpu.VMEM((width, ff), bf16),
            pltpu.VMEM((width, ff), bf16),
            pltpu.VMEM((ff, width), bf16),
            pltpu.VMEM((n_group * cap, width), bf16),
            pltpu.VMEM((n_group * cap, LANES), bf16),
            pltpu.VMEM((n_tok, n_group * cap), bf16),
            pltpu.VMEM((chunks, 4 * n1, width), bf16),
            pltpu.VMEM((chunks, nb, cap, LANES), bf16),
            pltpu.VMEM((chunks, 4, cap, LANES), bf16),
            pltpu.VMEM((4 * n1, LANES), jnp.float32),
            pltpu.VMEM((4 * n1, ff), bf16),
            pltpu.VMEM((chunks, 4 * n1, width), bf16),
            pltpu.VMEM((chunks, 2, n1 // 2, width), bf16),
            pltpu.VMEM((chunks, 2, n1, width), bf16),
            pltpu.VMEM((chunks, n1, width), bf16),
            pltpu.VMEM((n_group * cap, width), bf16),
            pltpu.SemaphoreType.REGULAR((ring_z // 2,)),
            dma((3,)),
            dma((n_group,)), dma((n_group,)),
            dma((n_group,)), dma((n_group,)),
            dma((chunks, 2)), dma((chunks, 2)),
            dma((chunks, 2)), dma((chunks, 2)),
            dma((chunks, 3)), dma((chunks, 3)),
            dma((chunks, 2)), dma((chunks, 2)),
            dma((chunks, 4)), dma((chunks, 4)),
            dma((n_group,)), dma((n_group,)),
        ],
        compiler_params=pltpu.CompilerParams(
            collective_id=0, has_side_effects=True, vmem_limit_bytes=60 * 1024 * 1024
        ),
        name="moe_layer",
    )(tokens, expert_ids.T, gates.T, w_gate, w_up, w_down)


def solution(mesh):
    in_specs = (
        P(("rep", "group", "local"), None),
        P(("rep", "group", "local"), None),
        P(("rep", "group", "local"), None),
        P(("group", "local"), None, None),
        P(("group", "local"), None, None),
        P(("group", "local"), None, None),
    )
    out_specs = P(("rep", "group", "local"), None)
    return jax.shard_map(
        functools.partial(shards, RING_Z, BLOCKS_CHUNK),
        mesh=mesh, in_specs=in_specs, out_specs=out_specs, check_vma=False,
    )
```

```python
import functools

import jax
import jax.numpy as jnp
from jax import lax
from jax.experimental import pallas as pl
from jax.experimental.pallas import tpu as pltpu
from jax.sharding import PartitionSpec as P

MESH = pl.DeviceIdType.MESH
GROUPS_TOK = 4
RING_Z = 8
LANES = 128
PREPARE = (1, 2)
LAGS = (1, 3, 4, 5)
BLOCKS_CHUNK = 4


def tile_of(size, most):
    tile = min(size, most)
    while size % tile:
        tile -= LANES
    return tile


def layer_kernel(
    cfg,
    tok_ref, ids_ref, gates_ref, wg_hbm, wu_hbm, wd_hbm,
    out_ref,
    wg, wu, wd, route_in, tok_in, places, sent, sent_gates, place_ref, rows, gates_in, packed, wcol, hidden, part, half_in, full_in, back, returned,
    wide_sem, w_sem, t_send, t_recv, s_send, s_recv, a_send, a_recv, h_send, h_recv, d_send, d_recv, f_send, f_recv, g_send, g_recv, p_send, p_recv, q_send, q_recv, b_send, b_recv,
):
    n_group, cap, nz, nb, chunks, width, ff = cfg
    nx = n_group // nz
    n_tok = tok_ref.shape[0]
    part_rows = nb * cap
    half = part_rows // 2
    slots = n_group * cap
    f32, bf16 = jnp.float32, jnp.bfloat16

    me = lax.axis_index("group")
    mx, mz = me // nz, lax.rem(me, nz)
    my = lax.axis_index("local")
    right, left = lax.rem(my + 1, 4), lax.rem(my + 3, 4)

    full_size = (nx, nz) == (4, 8) and nb == 4

    def chunk_of(p):
        return lax.rem(p + 2, chunks) if full_size else p

    def is_far(c):
        return (c >= 2) & (c <= 6) if full_size else c >= 1

    n_near = 3 if full_size else 1
    far_blocks = (2 * nb, 7 * nb) if full_size else (nb, n_group)

    def near_chunk(i):
        return i + 5 * (i // 2) if full_size else i

    def near_index(c):
        return c - 5 * (c // 7) if full_size else c

    def lane_block(group):
        dx, dz = lax.rem(group // nz + nx - mx, nx), lax.rem(lax.rem(group, nz) + nz - mz, nz)
        if (nx, nz) != (4, 8):
            return lax.rem(dx * nz + dz, nb)
        split = jnp.minimum(lax.rem(dz, 4), 1)
        b = (1 - split) * dx + split * (2 * lax.rem(dx, 2) + dz // 4)
        return b

    def offset(j):
        if (nx, nz) != (4, 8):
            return j // nz, lax.rem(j, nz)
        c, b = j // 4, lax.rem(j, 4)
        both = (lax.rem(c, 4) + 3) // 4
        dx = (1 - both) * b + both * (b // 2 + 2 * (c // 4))
        return dx, (4 - jnp.abs(c - 4)) * (1 - 2 * lax.rem(b, 2))

    def forth(j):
        dx, dz = offset(j)
        return lax.rem(mx + dx, nx) * nz + lax.rem(mz + dz + nz, nz)

    def origin(j):
        dx, dz = offset(j)
        return lax.rem(mx - dx + nx, nx) * nz + lax.rem(mz - dz + nz, nz)

    barrier = pltpu.get_barrier_semaphore()

    def at_group(dx, dz):
        return {"group": lax.rem(mx + dx, nx) * nz + lax.rem(mz + dz, nz)}

    ring = sorted({1, nz - 1})
    near_by = [at_group(dx, 0) for dx in range(1, nx)] + [at_group(0, dz) for dz in ring]
    near_by += [{"local": right}, {"local": left}]
    for device in near_by:
        pl.semaphore_signal(barrier, inc=1, device_id=device, device_id_type=MESH)

    def tell(k):
        for dz in ring:
            pl.semaphore_signal(wide_sem.at[k], inc=1, device_id=at_group(0, dz), device_id_type=MESH)

    def hear(k):
        pl.semaphore_wait(wide_sem.at[k], len(ring))

    loads = [
        pltpu.make_async_copy(hbm.at[0], vmem, w_sem.at[i])
        for i, (hbm, vmem) in enumerate(((wg_hbm, wg), (wu_hbm, wu), (wd_hbm, wd)))
    ]
    for load in loads:
        load.start()

    top = ids_ref.shape[0]
    route_in[0] = jnp.zeros_like(route_in[0])
    route_in[0, pl.ds(0, top), pl.ds(0, n_tok)] = ids_ref[...].astype(f32).astype(bf16)
    route_in[0, pl.ds(top, top), pl.ds(0, n_tok)] = gates_ref[...]

    expert_at = lax.broadcasted_iota(jnp.int32, (LANES, n_tok), 0).astype(f32)
    slot_at = lax.broadcasted_iota(jnp.int32, (slots, LANES), 0)
    of_expert = lax.broadcasted_iota(jnp.int32, (slots, LANES), 1)
    in_group = jnp.where(slot_at // cap == of_expert // 4, 1.0, 0.0).astype(bf16)
    t_row = lax.broadcasted_iota(jnp.int32, (n_tok, n_tok), 0)
    t_col = lax.broadcasted_iota(jnp.int32, (n_tok, n_tok), 1)
    before = jnp.where(t_row < t_col, 1.0, 0.0).astype(bf16)
    slot_rank = lax.rem(lax.broadcasted_iota(jnp.int32, (slots, n_tok), 0), cap).astype(f32)
    across = (((1,), (1,)), ((), ()))
    same_tok = jnp.where(t_row == t_col, 1.0, 0.0).astype(bf16)
    e_row = lax.broadcasted_iota(jnp.int32, (LANES, LANES), 0)
    e_lane = lax.broadcasted_iota(jnp.int32, (LANES, LANES), 1)
    to_lane = jnp.where(e_lane == lane_block(e_row // 4) * 4 + lax.rem(e_row, 4), 1.0, 0.0).astype(bf16)
    cols = tile_of(width, 512)

    def route(r):
        hit = jnp.zeros((LANES, n_tok), f32)
        weight = jnp.zeros((LANES, n_tok), f32)
        for k in range(top):
            same = route_in[r, k : k + 1, :n_tok].astype(f32) == expert_at
            hit = jnp.where(same, 1.0, hit)
            weight = jnp.where(same, route_in[r, top + k : top + k + 1, :n_tok].astype(f32), weight)
        count = jnp.dot(in_group, hit.astype(bf16), preferred_element_type=f32)
        member = jnp.where(count > 0.5, 1.0, 0.0)
        rank = jnp.dot(member.astype(bf16), before, preferred_element_type=f32)
        place = jnp.where((count > 0.5) & (rank == slot_rank), 1.0, 0.0).astype(bf16)
        places[r] = place
        of_slot = lax.dot_general(place, weight.astype(bf16), across, preferred_element_type=f32).astype(bf16)
        moved = jnp.dot(of_slot * in_group, to_lane, preferred_element_type=f32)
        sent_gates[:, r] = moved.reshape(n_group, cap, LANES).astype(bf16)
        return place

    def fill(r):
        def gather_cols(n, carry):
            at = pl.ds(pl.multiple_of(n * cols, cols), cols)
            tok = tok_ref[:, at] if r == 0 else tok_in[r, :, at]
            sent[r, :, at] = jnp.dot(places[r], tok, preferred_element_type=f32).astype(bf16)
            return carry

        lax.fori_loop(0, width // cols, gather_cols, 0)

    def block(ref, index):
        return ref.at[pl.ds(pl.multiple_of(index * cap, cap), cap), :]

    def dispatch(j):
        target = forth(j)
        return pltpu.make_async_remote_copy(
            src_ref=block(sent.at[0], target),
            dst_ref=block(rows.at[j // nb], lax.rem(j, nb)),
            send_sem=a_send.at[j],
            recv_sem=a_recv.at[j],
            device_id={"group": target},
            device_id_type=MESH,
        )

    def gates_copy(j, far_chunk):
        target = forth(j)
        at = (j // nb, lax.rem(j, nb)) + ((0,) if far_chunk else ())
        return pltpu.make_async_remote_copy(
            src_ref=sent_gates.at[target, 0] if far_chunk else sent_gates.at[target],
            dst_ref=gates_in.at[at],
            send_sem=h_send.at[j],
            recv_sem=h_recv.at[j],
            device_id={"group": target},
            device_id_type=MESH,
        )

    def near_copy(i, r):
        j = near_chunk(i // nb) * nb + lax.rem(i, nb)
        target = forth(j)
        return pltpu.make_async_remote_copy(
            src_ref=block(sent.at[r], target),
            dst_ref=block(rows.at[j // nb], r * nb + lax.rem(j, nb)),
            send_sem=s_send.at[i, r],
            recv_sem=s_recv.at[i, r],
            device_id={"group": target},
            device_id_type=MESH,
        )

    def near_rows(r):
        pltpu.make_async_copy(block(sent.at[r], me), block(rows.at[0], r * nb), s_recv.at[0, r]).start()

        def one(i, carry):
            near_copy(i, r).start()
            return carry

        lax.fori_loop(1, n_near * nb, one, 0)

    def near_gates():
        pltpu.make_async_copy(sent_gates.at[me], gates_in.at[0, 0], h_recv.at[0]).start()

        def one(i, carry):
            gates_copy(near_chunk(i // nb) * nb + lax.rem(i, nb), False).start()
            return carry

        lax.fori_loop(1, n_near * nb, one, 0)

    def give_back(j):
        return pltpu.make_async_remote_copy(
            src_ref=block(back.at[j // nb], lax.rem(j, nb)),
            dst_ref=block(returned, me),
            send_sem=b_send.at[j],
            recv_sem=b_recv.at[j],
            device_id={"group": origin(j)},
            device_id_type=MESH,
        )

    def copy_y(src, dst, send, recv, side):
        return pltpu.make_async_remote_copy(
            src_ref=src, dst_ref=dst, send_sem=send, recv_sem=recv,
            device_id={"local": right if side == 0 else left}, device_id_type=MESH,
        )

    hn = n_tok // 2

    def tile_direct(side):
        return copy_y(route_in.at[0], route_in.at[(3, 1)[side]], t_send.at[side], t_recv.at[side], side)

    def tile_onward():
        return copy_y(route_in.at[3], route_in.at[2], t_send.at[2], t_recv.at[2], 0)

    def tok_direct(side, second):
        at = pl.ds(hn if (side == 0) == second else 0, hn)
        k = 3 + 2 * side + int(second)
        return copy_y(tok_ref.at[at, :], tok_in.at[(3, 1)[side], at, :], t_send.at[k], t_recv.at[k], side)

    def tok_onward(side):
        at = pl.ds((0, hn)[side], hn)
        return copy_y(tok_in.at[(3, 1)[side], at, :], tok_in.at[2, at, :], t_send.at[7 + side], t_recv.at[7 + side], side)

    pl.semaphore_wait(barrier, len(near_by))
    for side in (0, 1):
        tile_direct(side).start()
    for side in (0, 1):
        tok_direct(side, False).start()
    for side in (0, 1):
        tok_direct(side, True).start()
    tell(0)
    place_ref[...] = lax.dot_general(same_tok, route(0), across, preferred_element_type=f32).astype(bf16)
    fill(0)

    def start_far(j, carry):
        dispatch(j).start()
        gates_copy(j, True).start()
        return carry

    done = far_blocks[0]
    for k in range(nz // 2):
        hear(k)
        if k + 1 < nz // 2:
            tell(k + 1)
        reach = far_blocks[1] if k + 1 == nz // 2 else nb * (k + 2) if full_size else done
        if reach > done:
            lax.fori_loop(done, reach, start_far, 0)
        done = max(done, reach)
    near_rows(0)

    def piece(ref, c, begin, size):
        return ref.at[c, pl.ds(begin, size), :]

    n1, n2, n3 = part_rows, 2 * part_rows, 3 * part_rows

    def direct(c, side):
        return copy_y(piece(rows, c, 0, n1), piece(rows, c, (n3, n1)[side], n1),
                      d_send.at[c, side], d_recv.at[c, side], side)

    def onward(c, side):
        return copy_y(piece(rows, c, (n3, n1 + half)[side], half), piece(rows, c, (n2, n2 + half)[side], half),
                      f_send.at[c, side], f_recv.at[c, side], side)

    def direct_weights(c, side):
        return copy_y(packed.at[c, 0], packed.at[c, (3, 1)[side]], g_send.at[c, side], g_recv.at[c, side], side)

    def onward_weights(c):
        return copy_y(packed.at[c, 3], packed.at[c, 2], g_send.at[c, 2], g_recv.at[c, 2], 0)

    def far(c, side):
        return copy_y(piece(part, c, (n2, n2 + half)[side], half), half_in.at[c, side],
                      p_send.at[c, side], p_recv.at[c, side], side)

    def near(c, side, which):
        begin = (half if which == 0 else 0) if side == 0 else (0 if which == 0 else half)
        return copy_y(piece(part, c, (n1, n3)[side] + begin, half), full_in.at[c, side, pl.ds(begin, half), :],
                      q_send.at[c, 2 * which + side], q_recv.at[c, 2 * which + side], side)

    fcols = tile_of(ff, 256)
    dcols = tile_of(width, 512)

    def compute(c):
        lane = lax.broadcasted_iota(jnp.int32, (cap, LANES), 1)
        for r in range(4):
            gate_of = packed[c, r].astype(f32)
            for b in range(nb):
                mine = jnp.sum(jnp.where(lane == b * 4 + my, gate_of, 0.0), axis=1, keepdims=True)
                wcol[pl.ds(r * part_rows + b * cap, cap), :] = jnp.broadcast_to(mine, (cap, LANES))

        def up_cols(n, carry):
            at = pl.ds(pl.multiple_of(n * fcols, fcols), fcols)
            x = rows[c]
            gate = jnp.dot(x, wg[:, at], preferred_element_type=f32)
            up = jnp.dot(x, wu[:, at], preferred_element_type=f32)
            hidden[:, at] = (gate / (1.0 + jnp.exp(-gate)) * up).astype(bf16)
            return carry

        lax.fori_loop(0, ff // fcols, up_cols, 0)

        def down_cols(n, carry):
            at = pl.ds(pl.multiple_of(n * dcols, dcols), dcols)
            value = jnp.dot(hidden[...], wd[:, at], preferred_element_type=f32)
            part[c, :, at] = (value * wcol[:, 0:1]).astype(bf16)
            return carry

        lax.fori_loop(0, width // dcols, down_cols, 0)

    def step(s, carry):
        first = chunk_of(jnp.minimum(s, chunks - 1))

        @pl.when((s < chunks) & is_far(first))
        def _():
            c = first

            def arrived(b, inner):
                j = c * nb + b
                pltpu.make_async_copy(block(sent.at[0], 0), block(rows.at[c], b), a_recv.at[j]).wait()
                pltpu.make_async_copy(sent_gates.at[0, 0], gates_in.at[c, b, 0], h_recv.at[j]).wait()
                return inner

            lax.fori_loop(0, nb, arrived, 0)
            packed[c, 0] = jnp.sum(gates_in[c, :, 0].astype(f32), axis=0).astype(bf16)
            for side in (0, 1):
                direct(c, side).start()
            for side in (0, 1):
                direct_weights(c, side).start()

        @pl.when(s == 0)
        def _():
            for side in (0, 1):
                tok_direct(side, False).wait_recv()
                tok_onward(side).start()
            for side in (0, 1):
                tile_direct(side).wait_recv()
            tile_onward().start()

        second = chunk_of(jnp.clip(s - LAGS[0], 0, chunks - 1))

        @pl.when((s >= LAGS[0]) & (s < chunks + LAGS[0]) & is_far(second))
        def _():
            c = second
            for side in (0, 1):
                direct(c, side).wait_recv()
                onward(c, side).start()
            for side in (0, 1):
                direct_weights(c, side).wait_recv()
            onward_weights(c).start()

        @pl.when(s == PREPARE[0])
        def _():
            for side in (0, 1):
                tok_direct(side, True).wait_recv()
                r = (3, 1)[side]
                route(r)
                fill(r)
                near_rows(r)

        @pl.when(s == PREPARE[1])
        def _():
            for side in (0, 1):
                tok_onward(side).wait_recv()
            tile_onward().wait_recv()
            route(2)
            fill(2)
            near_rows(2)
            near_gates()

        @pl.when((s >= LAGS[1]) & (s < chunks + LAGS[1]))
        def _():
            c = chunk_of(s - LAGS[1])

            @pl.when(s == LAGS[1])
            def _():
                for load in loads:
                    load.wait()

            @pl.when(is_far(c))
            def _():
                for side in (0, 1):
                    onward(c, side).wait_recv()
                onward_weights(c).wait_recv()

            @pl.when(jnp.logical_not(is_far(c)))
            def _():
                def arrived(b, inner):
                    for r in range(4):
                        pltpu.make_async_copy(
                            block(sent.at[r], 0), block(rows.at[c], r * nb + b), s_recv.at[near_index(c) * nb + b, r]
                        ).wait()
                    pltpu.make_async_copy(sent_gates.at[0], gates_in.at[c, b], h_recv.at[c * nb + b]).wait()
                    return inner

                lax.fori_loop(0, nb, arrived, 0)
                packed[c] = jnp.sum(gates_in[c].astype(f32), axis=0).astype(bf16)

            compute(c)
            for side in (0, 1):
                far(c, side).start()
            for side in (0, 1):
                near(c, side, 0).start()

        @pl.when((s >= LAGS[2]) & (s < chunks + LAGS[2]))
        def _():
            c = chunk_of(s - LAGS[2])
            for side in (0, 1):
                far(c, side).wait_recv()
                at = pl.ds((n1, n3 + half)[side], half)
                part[c, at, :] = (part[c, at, :].astype(f32) + half_in[c, side].astype(f32)).astype(bf16)
                near(c, side, 1).start()

        @pl.when(s >= LAGS[3])
        def _():
            c = chunk_of(s - LAGS[3])
            for which in (0, 1):
                for side in (0, 1):
                    near(c, side, which).wait_recv()
            back[c] = (
                part[c, pl.ds(0, n1), :].astype(f32)
                + full_in[c, 0].astype(f32)
                + full_in[c, 1].astype(f32)
            ).astype(bf16)

            def send_back(b, inner):
                j = c * nb + b

                @pl.when(j == 0)
                def _():
                    pltpu.make_async_copy(block(back.at[0], 0), block(returned, me), b_recv.at[0]).start()

                @pl.when(j != 0)
                def _():
                    give_back(j).start()

                return inner

            lax.fori_loop(0, nb, send_back, 0)

        return carry

    lax.fori_loop(0, chunks + LAGS[3], step, 0)

    def sends_done(c, carry):
        @pl.when(is_far(c))
        def _():
            for side in (0, 1):
                direct(c, side).wait_send()
                direct_weights(c, side).wait_send()
                onward(c, side).wait_send()
            onward_weights(c).wait_send()

        for side in (0, 1):
            far(c, side).wait_send()
            near(c, side, 0).wait_send()
            near(c, side, 1).wait_send()
        return carry

    lax.fori_loop(0, chunks, sends_done, 0)
    for side in (0, 1):
        tile_direct(side).wait_send()
        tok_direct(side, False).wait_send()
        tok_direct(side, True).wait_send()
        tok_onward(side).wait_send()
    tile_onward().wait_send()

    def far_sent(j, carry):
        dispatch(j).wait_send()
        gates_copy(j, True).wait_send()
        return carry

    lax.fori_loop(*far_blocks, far_sent, 0)

    def near_sent(i, carry):
        for r in range(4):
            near_copy(i, r).wait_send()
        gates_copy(near_chunk(i // nb) * nb + lax.rem(i, nb), False).wait_send()
        return carry

    lax.fori_loop(1, n_near * nb, near_sent, 0)

    def blocks_done(j, carry):
        give_back(j).wait_send()
        return carry

    lax.fori_loop(1, n_group, blocks_done, 0)

    def came_back(j, carry):
        pltpu.make_async_copy(block(back.at[0], 0), block(returned, forth(j)), b_recv.at[j]).wait()
        return carry

    lax.fori_loop(0, n_group, came_back, 0)

    def mix_cols(n, carry):
        at = pl.ds(pl.multiple_of(n * cols, cols), cols)
        out_ref[:, at] = jnp.dot(place_ref[...], returned[:, at], preferred_element_type=f32).astype(bf16)
        return carry

    lax.fori_loop(0, width // cols, mix_cols, 0)


def shards(ring_z, blocks_chunk, tokens, gates, expert_ids, w_gate, w_up, w_down):
    n_tok, width = tokens.shape
    n_group = lax.axis_size("group")
    ff = w_gate.shape[2]
    cap = min(n_tok, n_tok * GROUPS_TOK // n_group)
    nb = blocks_chunk
    chunks = n_group // nb
    n1 = nb * cap
    bf16 = jnp.bfloat16
    vmem = pl.BlockSpec(memory_space=pltpu.VMEM)
    hbm = pl.BlockSpec(memory_space=pl.ANY)
    dma = pltpu.SemaphoreType.DMA
    cfg = (n_group, cap, ring_z, nb, chunks, width, ff)
    return pl.pallas_call(
        functools.partial(layer_kernel, cfg),
        out_shape=jax.ShapeDtypeStruct((n_tok, width), bf16),
        in_specs=[vmem, vmem, vmem, hbm, hbm, hbm],
        out_specs=vmem,
        scratch_shapes=[
            pltpu.VMEM((width, ff), bf16),
            pltpu.VMEM((width, ff), bf16),
            pltpu.VMEM((ff, width), bf16),
            pltpu.VMEM((4, 2 * expert_ids.shape[1], LANES), bf16),
            pltpu.VMEM((4, n_tok, width), bf16),
            pltpu.VMEM((4, n_group * cap, n_tok), bf16),
            pltpu.VMEM((4, n_group * cap, width), bf16),
            pltpu.VMEM((n_group, 4, cap, LANES), bf16),
            pltpu.VMEM((n_tok, n_group * cap), bf16),
            pltpu.VMEM((chunks, 4 * n1, width), bf16),
            pltpu.VMEM((chunks, nb, 4, cap, LANES), bf16),
            pltpu.VMEM((chunks, 4, cap, LANES), bf16),
            pltpu.VMEM((4 * n1, LANES), jnp.float32),
            pltpu.VMEM((4 * n1, ff), bf16),
            pltpu.VMEM((chunks, 4 * n1, width), bf16),
            pltpu.VMEM((chunks, 2, n1 // 2, width), bf16),
            pltpu.VMEM((chunks, 2, n1, width), bf16),
            pltpu.VMEM((chunks, n1, width), bf16),
            pltpu.VMEM((n_group * cap, width), bf16),
            pltpu.SemaphoreType.REGULAR((ring_z // 2,)),
            dma((3,)),
            dma((9,)), dma((9,)),
            dma((3 * nb, 4)), dma((3 * nb, 4)),
            dma((n_group,)), dma((n_group,)),
            dma((n_group,)), dma((n_group,)),
            dma((chunks, 2)), dma((chunks, 2)),
            dma((chunks, 2)), dma((chunks, 2)),
            dma((chunks, 3)), dma((chunks, 3)),
            dma((chunks, 2)), dma((chunks, 2)),
            dma((chunks, 4)), dma((chunks, 4)),
            dma((n_group,)), dma((n_group,)),
        ],
        compiler_params=pltpu.CompilerParams(
            collective_id=0, has_side_effects=True, vmem_limit_bytes=60 * 1024 * 1024
        ),
        name="moe_layer",
    )(tokens, expert_ids.T, gates.T, w_gate, w_up, w_down)


def solution(mesh):
    in_specs = (
        P(("rep", "group", "local"), None),
        P(("rep", "group", "local"), None),
        P(("rep", "group", "local"), None),
        P(("group", "local"), None, None),
        P(("group", "local"), None, None),
        P(("group", "local"), None, None),
    )
    out_specs = P(("rep", "group", "local"), None)
    return jax.shard_map(
        functools.partial(shards, RING_Z, BLOCKS_CHUNK),
        mesh=mesh, in_specs=in_specs, out_specs=out_specs, check_vma=False,
    )
```

```python
import functools

import jax
import jax.numpy as jnp
from jax import lax
from jax.experimental import pallas as pl
from jax.experimental.pallas import tpu as pltpu
from jax.sharding import PartitionSpec as P

MESH = pl.DeviceIdType.MESH
GROUPS_TOK = 4
RING_Z = 8
LANES = 128
PREPARE = (1, 2)
LAGS = (1, 3, 4, 5)
BLOCKS_CHUNK = 4


def tile_of(size, most):
    tile = min(size, most)
    while size % tile:
        tile -= LANES
    return tile


def layer_kernel(
    cfg,
    tok_ref, ids_ref, gates_ref, wg_hbm, wu_hbm, wd_hbm,
    out_ref,
    wg, wu, wd, route_in, tok_in, places, sent, sent_gates, place_ref, rows, gates_in, packed, wcol, hidden, part, half_in, full_in, back, returned,
    wide_sem, w_sem, t_send, t_recv, s_send, s_recv, a_send, a_recv, h_send, h_recv, d_send, d_recv, f_send, f_recv, g_send, g_recv, p_send, p_recv, q_send, q_recv, b_send, b_recv,
):
    n_group, cap, nz, nb, chunks, width, ff = cfg
    nx = n_group // nz
    n_tok = tok_ref.shape[0]
    part_rows = nb * cap
    half = part_rows // 2
    slots = n_group * cap
    f32, bf16 = jnp.float32, jnp.bfloat16

    me = lax.axis_index("group")
    mx, mz = me // nz, lax.rem(me, nz)
    my = lax.axis_index("local")
    right, left = lax.rem(my + 1, 4), lax.rem(my + 3, 4)

    full_size = (nx, nz) == (4, 8) and nb == 4

    def chunk_of(p):
        return lax.rem(p + 2, chunks) if full_size else p

    def is_far(c):
        return (c >= 2) & (c <= 6) if full_size else c >= 1

    n_near = 3 if full_size else 1
    far_blocks = (2 * nb, 7 * nb) if full_size else (nb, n_group)

    def near_chunk(i):
        return i + 5 * (i // 2) if full_size else i

    def near_index(c):
        return c - 5 * (c // 7) if full_size else c

    def lane_block(group):
        dx, dz = lax.rem(group // nz + nx - mx, nx), lax.rem(lax.rem(group, nz) + nz - mz, nz)
        if (nx, nz) != (4, 8):
            return lax.rem(dx * nz + dz, nb)
        split = jnp.minimum(lax.rem(dz, 4), 1)
        b = (1 - split) * dx + split * (2 * lax.rem(dx, 2) + dz // 4)
        return b

    def offset(j):
        if (nx, nz) != (4, 8):
            return j // nz, lax.rem(j, nz)
        c, b = j // 4, lax.rem(j, 4)
        both = (lax.rem(c, 6) + 5) // 6
        dx = (1 - both) * b + both * (b // 2 + 2 * lax.rem(c, 2) * ((c + 2) // 5))
        away = (c + 2) // 2 - (7 - c) // 7 - 3 * (c // 7)
        return dx, away * (1 - 2 * lax.rem(b, 2))

    def forth(j):
        dx, dz = offset(j)
        return lax.rem(mx + dx, nx) * nz + lax.rem(mz + dz + nz, nz)

    def origin(j):
        dx, dz = offset(j)
        return lax.rem(mx - dx + nx, nx) * nz + lax.rem(mz - dz + nz, nz)

    barrier = pltpu.get_barrier_semaphore()

    def at_group(dx, dz):
        return {"group": lax.rem(mx + dx, nx) * nz + lax.rem(mz + dz, nz)}

    ring = sorted({1, nz - 1})
    near_by = [at_group(dx, 0) for dx in range(1, nx)] + [at_group(0, dz) for dz in ring]
    near_by += [{"local": right}, {"local": left}]
    for device in near_by:
        pl.semaphore_signal(barrier, inc=1, device_id=device, device_id_type=MESH)

    def tell(k):
        for dz in ring:
            pl.semaphore_signal(wide_sem.at[k], inc=1, device_id=at_group(0, dz), device_id_type=MESH)

    def hear(k):
        pl.semaphore_wait(wide_sem.at[k], len(ring))

    loads = [
        pltpu.make_async_copy(hbm.at[0], vmem, w_sem.at[i])
        for i, (hbm, vmem) in enumerate(((wg_hbm, wg), (wu_hbm, wu), (wd_hbm, wd)))
    ]
    for load in loads:
        load.start()

    top = ids_ref.shape[0]
    route_in[0] = jnp.zeros_like(route_in[0])
    route_in[0, pl.ds(0, top), pl.ds(0, n_tok)] = ids_ref[...].astype(f32).astype(bf16)
    route_in[0, pl.ds(top, top), pl.ds(0, n_tok)] = gates_ref[...]

    expert_at = lax.broadcasted_iota(jnp.int32, (LANES, n_tok), 0).astype(f32)
    slot_at = lax.broadcasted_iota(jnp.int32, (slots, LANES), 0)
    of_expert = lax.broadcasted_iota(jnp.int32, (slots, LANES), 1)
    in_group = jnp.where(slot_at // cap == of_expert // 4, 1.0, 0.0).astype(bf16)
    t_row = lax.broadcasted_iota(jnp.int32, (n_tok, n_tok), 0)
    t_col = lax.broadcasted_iota(jnp.int32, (n_tok, n_tok), 1)
    before = jnp.where(t_row < t_col, 1.0, 0.0).astype(bf16)
    slot_rank = lax.rem(lax.broadcasted_iota(jnp.int32, (slots, n_tok), 0), cap).astype(f32)
    across = (((1,), (1,)), ((), ()))
    same_tok = jnp.where(t_row == t_col, 1.0, 0.0).astype(bf16)
    e_row = lax.broadcasted_iota(jnp.int32, (LANES, LANES), 0)
    e_lane = lax.broadcasted_iota(jnp.int32, (LANES, LANES), 1)
    to_lane = jnp.where(e_lane == lane_block(e_row // 4) * 4 + lax.rem(e_row, 4), 1.0, 0.0).astype(bf16)
    cols = tile_of(width, 512)

    def route(r):
        hit = jnp.zeros((LANES, n_tok), f32)
        weight = jnp.zeros((LANES, n_tok), f32)
        for k in range(top):
            same = route_in[r, k : k + 1, :n_tok].astype(f32) == expert_at
            hit = jnp.where(same, 1.0, hit)
            weight = jnp.where(same, route_in[r, top + k : top + k + 1, :n_tok].astype(f32), weight)
        count = jnp.dot(in_group, hit.astype(bf16), preferred_element_type=f32)
        member = jnp.where(count > 0.5, 1.0, 0.0)
        rank = jnp.dot(member.astype(bf16), before, preferred_element_type=f32)
        place = jnp.where((count > 0.5) & (rank == slot_rank), 1.0, 0.0).astype(bf16)
        places[r] = place
        of_slot = lax.dot_general(place, weight.astype(bf16), across, preferred_element_type=f32).astype(bf16)
        moved = jnp.dot(of_slot * in_group, to_lane, preferred_element_type=f32)
        sent_gates[:, r] = moved.reshape(n_group, cap, LANES).astype(bf16)
        return place

    def fill(r):
        def gather_cols(n, carry):
            at = pl.ds(pl.multiple_of(n * cols, cols), cols)
            tok = tok_ref[:, at] if r == 0 else tok_in[r, :, at]
            sent[r, :, at] = jnp.dot(places[r], tok, preferred_element_type=f32).astype(bf16)
            return carry

        lax.fori_loop(0, width // cols, gather_cols, 0)

    def block(ref, index):
        return ref.at[pl.ds(pl.multiple_of(index * cap, cap), cap), :]

    def dispatch(j):
        target = forth(j)
        return pltpu.make_async_remote_copy(
            src_ref=block(sent.at[0], target),
            dst_ref=block(rows.at[j // nb], lax.rem(j, nb)),
            send_sem=a_send.at[j],
            recv_sem=a_recv.at[j],
            device_id={"group": target},
            device_id_type=MESH,
        )

    def gates_copy(j, far_chunk):
        target = forth(j)
        at = (j // nb, lax.rem(j, nb)) + ((0,) if far_chunk else ())
        return pltpu.make_async_remote_copy(
            src_ref=sent_gates.at[target, 0] if far_chunk else sent_gates.at[target],
            dst_ref=gates_in.at[at],
            send_sem=h_send.at[j],
            recv_sem=h_recv.at[j],
            device_id={"group": target},
            device_id_type=MESH,
        )

    def near_copy(i, r):
        j = near_chunk(i // nb) * nb + lax.rem(i, nb)
        target = forth(j)
        return pltpu.make_async_remote_copy(
            src_ref=block(sent.at[r], target),
            dst_ref=block(rows.at[j // nb], r * nb + lax.rem(j, nb)),
            send_sem=s_send.at[i, r],
            recv_sem=s_recv.at[i, r],
            device_id={"group": target},
            device_id_type=MESH,
        )

    def near_rows(r):
        pltpu.make_async_copy(block(sent.at[r], me), block(rows.at[0], r * nb), s_recv.at[0, r]).start()

        def one(i, carry):
            near_copy(i, r).start()
            return carry

        lax.fori_loop(1, n_near * nb, one, 0)

    def near_gates():
        pltpu.make_async_copy(sent_gates.at[me], gates_in.at[0, 0], h_recv.at[0]).start()

        def one(i, carry):
            gates_copy(near_chunk(i // nb) * nb + lax.rem(i, nb), False).start()
            return carry

        lax.fori_loop(1, n_near * nb, one, 0)

    def give_back(j):
        return pltpu.make_async_remote_copy(
            src_ref=block(back.at[j // nb], lax.rem(j, nb)),
            dst_ref=block(returned, me),
            send_sem=b_send.at[j],
            recv_sem=b_recv.at[j],
            device_id={"group": origin(j)},
            device_id_type=MESH,
        )

    def copy_y(src, dst, send, recv, side):
        return pltpu.make_async_remote_copy(
            src_ref=src, dst_ref=dst, send_sem=send, recv_sem=recv,
            device_id={"local": right if side == 0 else left}, device_id_type=MESH,
        )

    hn = n_tok // 2

    def tile_direct(side):
        return copy_y(route_in.at[0], route_in.at[(3, 1)[side]], t_send.at[side], t_recv.at[side], side)

    def tile_onward():
        return copy_y(route_in.at[3], route_in.at[2], t_send.at[2], t_recv.at[2], 0)

    def tok_direct(side, second):
        at = pl.ds(hn if (side == 0) == second else 0, hn)
        k = 3 + 2 * side + int(second)
        return copy_y(tok_ref.at[at, :], tok_in.at[(3, 1)[side], at, :], t_send.at[k], t_recv.at[k], side)

    def tok_onward(side):
        at = pl.ds((0, hn)[side], hn)
        return copy_y(tok_in.at[(3, 1)[side], at, :], tok_in.at[2, at, :], t_send.at[7 + side], t_recv.at[7 + side], side)

    pl.semaphore_wait(barrier, len(near_by))
    for side in (0, 1):
        tile_direct(side).start()
    for side in (0, 1):
        tok_direct(side, False).start()
    for side in (0, 1):
        tok_direct(side, True).start()
    tell(0)
    place_ref[...] = lax.dot_general(same_tok, route(0), across, preferred_element_type=f32).astype(bf16)
    hear(0)
    if nz // 2 > 1:
        tell(1)
    fill(0)

    def start_far(j, carry):
        dispatch(j).start()
        gates_copy(j, True).start()
        return carry

    done = far_blocks[0]
    for k in range(nz // 2):
        if k:
            hear(k)
            if k + 1 < nz // 2:
                tell(k + 1)
        reach = far_blocks[1] if k + 1 == nz // 2 else 2 * nb * (k + 1) if full_size else done
        if reach > done:
            lax.fori_loop(done, reach, start_far, 0)
        done = max(done, reach)
    near_rows(0)

    def piece(ref, c, begin, size):
        return ref.at[c, pl.ds(begin, size), :]

    n1, n2, n3 = part_rows, 2 * part_rows, 3 * part_rows

    def direct(c, side):
        return copy_y(piece(rows, c, 0, n1), piece(rows, c, (n3, n1)[side], n1),
                      d_send.at[c, side], d_recv.at[c, side], side)

    def onward(c, side):
        return copy_y(piece(rows, c, (n3, n1 + half)[side], half), piece(rows, c, (n2, n2 + half)[side], half),
                      f_send.at[c, side], f_recv.at[c, side], side)

    def direct_weights(c, side):
        return copy_y(packed.at[c, 0], packed.at[c, (3, 1)[side]], g_send.at[c, side], g_recv.at[c, side], side)

    def onward_weights(c):
        return copy_y(packed.at[c, 3], packed.at[c, 2], g_send.at[c, 2], g_recv.at[c, 2], 0)

    def far(c, side):
        return copy_y(piece(part, c, (n2, n2 + half)[side], half), half_in.at[c, side],
                      p_send.at[c, side], p_recv.at[c, side], side)

    def near(c, side, which):
        begin = (half if which == 0 else 0) if side == 0 else (0 if which == 0 else half)
        return copy_y(piece(part, c, (n1, n3)[side] + begin, half), full_in.at[c, side, pl.ds(begin, half), :],
                      q_send.at[c, 2 * which + side], q_recv.at[c, 2 * which + side], side)

    fcols = tile_of(ff, 256)
    dcols = tile_of(width, 512)

    def compute(c):
        lane = lax.broadcasted_iota(jnp.int32, (cap, LANES), 1)
        for r in range(4):
            gate_of = packed[c, r].astype(f32)
            for b in range(nb):
                mine = jnp.sum(jnp.where(lane == b * 4 + my, gate_of, 0.0), axis=1, keepdims=True)
                wcol[pl.ds(r * part_rows + b * cap, cap), :] = jnp.broadcast_to(mine, (cap, LANES))

        def up_cols(n, carry):
            at = pl.ds(pl.multiple_of(n * fcols, fcols), fcols)
            x = rows[c]
            gate = jnp.dot(x, wg[:, at], preferred_element_type=f32)
            up = jnp.dot(x, wu[:, at], preferred_element_type=f32)
            hidden[:, at] = (gate / (1.0 + jnp.exp(-gate)) * up).astype(bf16)
            return carry

        lax.fori_loop(0, ff // fcols, up_cols, 0)

        def down_cols(n, carry):
            at = pl.ds(pl.multiple_of(n * dcols, dcols), dcols)
            value = jnp.dot(hidden[...], wd[:, at], preferred_element_type=f32)
            part[c, :, at] = (value * wcol[:, 0:1]).astype(bf16)
            return carry

        lax.fori_loop(0, width // dcols, down_cols, 0)

    def step(s, carry):
        first = chunk_of(jnp.minimum(s, chunks - 1))

        @pl.when((s < chunks) & is_far(first))
        def _():
            c = first

            def arrived(b, inner):
                j = c * nb + b
                pltpu.make_async_copy(block(sent.at[0], 0), block(rows.at[c], b), a_recv.at[j]).wait()
                pltpu.make_async_copy(sent_gates.at[0, 0], gates_in.at[c, b, 0], h_recv.at[j]).wait()
                return inner

            lax.fori_loop(0, nb, arrived, 0)
            packed[c, 0] = jnp.sum(gates_in[c, :, 0].astype(f32), axis=0).astype(bf16)
            for side in (0, 1):
                direct(c, side).start()
            for side in (0, 1):
                direct_weights(c, side).start()

        @pl.when(s == 0)
        def _():
            for side in (0, 1):
                tok_direct(side, False).wait_recv()
                tok_onward(side).start()
            for side in (0, 1):
                tile_direct(side).wait_recv()
            tile_onward().start()

        second = chunk_of(jnp.clip(s - LAGS[0], 0, chunks - 1))

        @pl.when((s >= LAGS[0]) & (s < chunks + LAGS[0]) & is_far(second))
        def _():
            c = second
            for side in (0, 1):
                direct(c, side).wait_recv()
                onward(c, side).start()
            for side in (0, 1):
                direct_weights(c, side).wait_recv()
            onward_weights(c).start()

        @pl.when(s == PREPARE[0])
        def _():
            for side in (0, 1):
                tok_direct(side, True).wait_recv()
                r = (3, 1)[side]
                route(r)
                fill(r)
                near_rows(r)

        @pl.when(s == PREPARE[1])
        def _():
            for side in (0, 1):
                tok_onward(side).wait_recv()
            tile_onward().wait_recv()
            route(2)
            fill(2)
            near_rows(2)
            near_gates()

        @pl.when((s >= LAGS[1]) & (s < chunks + LAGS[1]))
        def _():
            c = chunk_of(s - LAGS[1])

            @pl.when(s == LAGS[1])
            def _():
                for load in loads:
                    load.wait()

            @pl.when(is_far(c))
            def _():
                for side in (0, 1):
                    onward(c, side).wait_recv()
                onward_weights(c).wait_recv()

            @pl.when(jnp.logical_not(is_far(c)))
            def _():
                def arrived(b, inner):
                    for r in range(4):
                        pltpu.make_async_copy(
                            block(sent.at[r], 0), block(rows.at[c], r * nb + b), s_recv.at[near_index(c) * nb + b, r]
                        ).wait()
                    pltpu.make_async_copy(sent_gates.at[0], gates_in.at[c, b], h_recv.at[c * nb + b]).wait()
                    return inner

                lax.fori_loop(0, nb, arrived, 0)
                packed[c] = jnp.sum(gates_in[c].astype(f32), axis=0).astype(bf16)

            compute(c)
            for side in (0, 1):
                far(c, side).start()
            for side in (0, 1):
                near(c, side, 0).start()

        @pl.when((s >= LAGS[2]) & (s < chunks + LAGS[2]))
        def _():
            c = chunk_of(s - LAGS[2])
            for side in (0, 1):
                far(c, side).wait_recv()
                at = pl.ds((n1, n3 + half)[side], half)
                part[c, at, :] = (part[c, at, :].astype(f32) + half_in[c, side].astype(f32)).astype(bf16)
                near(c, side, 1).start()

        @pl.when(s >= LAGS[3])
        def _():
            c = chunk_of(s - LAGS[3])
            for which in (0, 1):
                for side in (0, 1):
                    near(c, side, which).wait_recv()
            back[c] = (
                part[c, pl.ds(0, n1), :].astype(f32)
                + full_in[c, 0].astype(f32)
                + full_in[c, 1].astype(f32)
            ).astype(bf16)

            def send_back(b, inner):
                j = c * nb + b

                @pl.when(j == 0)
                def _():
                    pltpu.make_async_copy(block(back.at[0], 0), block(returned, me), b_recv.at[0]).start()

                @pl.when(j != 0)
                def _():
                    give_back(j).start()

                return inner

            lax.fori_loop(0, nb, send_back, 0)

        return carry

    lax.fori_loop(0, chunks + LAGS[3], step, 0)

    def sends_done(c, carry):
        @pl.when(is_far(c))
        def _():
            for side in (0, 1):
                direct(c, side).wait_send()
                direct_weights(c, side).wait_send()
                onward(c, side).wait_send()
            onward_weights(c).wait_send()

        for side in (0, 1):
            far(c, side).wait_send()
            near(c, side, 0).wait_send()
            near(c, side, 1).wait_send()
        return carry

    lax.fori_loop(0, chunks, sends_done, 0)
    for side in (0, 1):
        tile_direct(side).wait_send()
        tok_direct(side, False).wait_send()
        tok_direct(side, True).wait_send()
        tok_onward(side).wait_send()
    tile_onward().wait_send()

    def far_sent(j, carry):
        dispatch(j).wait_send()
        gates_copy(j, True).wait_send()
        return carry

    lax.fori_loop(*far_blocks, far_sent, 0)

    def near_sent(i, carry):
        for r in range(4):
            near_copy(i, r).wait_send()
        gates_copy(near_chunk(i // nb) * nb + lax.rem(i, nb), False).wait_send()
        return carry

    lax.fori_loop(1, n_near * nb, near_sent, 0)

    def blocks_done(j, carry):
        give_back(j).wait_send()
        return carry

    lax.fori_loop(1, n_group, blocks_done, 0)

    def came_back(j, carry):
        pltpu.make_async_copy(block(back.at[0], 0), block(returned, forth(j)), b_recv.at[j]).wait()
        return carry

    lax.fori_loop(0, n_group, came_back, 0)

    def mix_cols(n, carry):
        at = pl.ds(pl.multiple_of(n * cols, cols), cols)
        out_ref[:, at] = jnp.dot(place_ref[...], returned[:, at], preferred_element_type=f32).astype(bf16)
        return carry

    lax.fori_loop(0, width // cols, mix_cols, 0)


def shards(ring_z, blocks_chunk, tokens, gates, expert_ids, w_gate, w_up, w_down):
    n_tok, width = tokens.shape
    n_group = lax.axis_size("group")
    ff = w_gate.shape[2]
    cap = min(n_tok, n_tok * GROUPS_TOK // n_group)
    nb = blocks_chunk
    chunks = n_group // nb
    n1 = nb * cap
    bf16 = jnp.bfloat16
    vmem = pl.BlockSpec(memory_space=pltpu.VMEM)
    hbm = pl.BlockSpec(memory_space=pl.ANY)
    dma = pltpu.SemaphoreType.DMA
    cfg = (n_group, cap, ring_z, nb, chunks, width, ff)
    return pl.pallas_call(
        functools.partial(layer_kernel, cfg),
        out_shape=jax.ShapeDtypeStruct((n_tok, width), bf16),
        in_specs=[vmem, vmem, vmem, hbm, hbm, hbm],
        out_specs=vmem,
        scratch_shapes=[
            pltpu.VMEM((width, ff), bf16),
            pltpu.VMEM((width, ff), bf16),
            pltpu.VMEM((ff, width), bf16),
            pltpu.VMEM((4, 2 * expert_ids.shape[1], LANES), bf16),
            pltpu.VMEM((4, n_tok, width), bf16),
            pltpu.VMEM((4, n_group * cap, n_tok), bf16),
            pltpu.VMEM((4, n_group * cap, width), bf16),
            pltpu.VMEM((n_group, 4, cap, LANES), bf16),
            pltpu.VMEM((n_tok, n_group * cap), bf16),
            pltpu.VMEM((chunks, 4 * n1, width), bf16),
            pltpu.VMEM((chunks, nb, 4, cap, LANES), bf16),
            pltpu.VMEM((chunks, 4, cap, LANES), bf16),
            pltpu.VMEM((4 * n1, LANES), jnp.float32),
            pltpu.VMEM((4 * n1, ff), bf16),
            pltpu.VMEM((chunks, 4 * n1, width), bf16),
            pltpu.VMEM((chunks, 2, n1 // 2, width), bf16),
            pltpu.VMEM((chunks, 2, n1, width), bf16),
            pltpu.VMEM((chunks, n1, width), bf16),
            pltpu.VMEM((n_group * cap, width), bf16),
            pltpu.SemaphoreType.REGULAR((ring_z // 2,)),
            dma((3,)),
            dma((9,)), dma((9,)),
            dma((3 * nb, 4)), dma((3 * nb, 4)),
            dma((n_group,)), dma((n_group,)),
            dma((n_group,)), dma((n_group,)),
            dma((chunks, 2)), dma((chunks, 2)),
            dma((chunks, 2)), dma((chunks, 2)),
            dma((chunks, 3)), dma((chunks, 3)),
            dma((chunks, 2)), dma((chunks, 2)),
            dma((chunks, 4)), dma((chunks, 4)),
            dma((n_group,)), dma((n_group,)),
        ],
        compiler_params=pltpu.CompilerParams(
            collective_id=0, has_side_effects=True, vmem_limit_bytes=60 * 1024 * 1024
        ),
        name="moe_layer",
    )(tokens, expert_ids.T, gates.T, w_gate, w_up, w_down)


def solution(mesh):
    in_specs = (
        P(("rep", "group", "local"), None),
        P(("rep", "group", "local"), None),
        P(("rep", "group", "local"), None),
        P(("group", "local"), None, None),
        P(("group", "local"), None, None),
        P(("group", "local"), None, None),
    )
    out_specs = P(("rep", "group", "local"), None)
    return jax.shard_map(
        functools.partial(shards, RING_Z, BLOCKS_CHUNK),
        mesh=mesh, in_specs=in_specs, out_specs=out_specs, check_vma=False,
    )
```
